1024 devices in a mesh: row: 32 (over x, y_hi), col: 32 (over z, y_lo, core).
Axes of the slice: x: 8, y: 8 (y_hi: 4, y_lo: 2; y = y_hi * 2 + y_lo), z: 8, core: 2. Of those that a mesh axis runs over, the one named last changes fastest.
Arguments:
- diag_inverse: bfloat16 [1376, 1376], P('row'), may hold values from -0.5 to 0.5, as said below
- row_u: bfloat16 [32, 1376, 224], P('row', None, 'col'), may hold values from -6 to 6
- row_v: bfloat16 [32, 1376, 224], P('row', None, 'col'), may hold values from -0.59765625 to 0.59765625
- col_u: bfloat16 [32, 1376, 224], P('col', None, 'row'), may hold values from -6 to 6
- col_v: bfloat16 [32, 1376, 224], P('col', None, 'row'), may hold values from -0.59765625 to 0.59765625
- tile_u: bfloat16 [32, 32, 1376, 224], P('row', 'col'), may hold values from -6 to 6
- tile_v: bfloat16 [32, 32, 1376, 224], P('row', 'col'), may hold values from -6 to 6
- sketch: bfloat16 [1376, 224], replicated, may hold values from -6 to 6
- row_rank: int32 [32], P('row'), may hold values from 56 to 224, as said below
- col_rank: int32 [32], P('col'), may hold values from 56 to 224, as said below
- old_rank: int32 [32, 32], P('row', 'col'), may hold values from 56 to 224, as said below
- new_rank: int32 [32, 32], P('row', 'col'), may hold values from 14 to 112, as said below
Outputs:
- new_u: bfloat16 [32, 32, 1376, 224], P('row', 'col')
- new_v: bfloat16 [32, 32, 1376, 224], P('row', 'col')
The draws below stay inside these ranges and needn't reach their ends.
Inputs may be any that keep to these rules, and one draw needn't show every extreme that they name: diag_inverse is lower triangular with diagonal entries between 0.25 and 0.5. `row_rank`: some tile has rank 224. `col_rank`: some tile has rank 224. `old_rank`: some tile has rank 224. `new_rank`: each entry lies between old_rank // 4 and old_rank // 2 of the same tile; some tile has rank 224 // 2.
All inputs are finite; a program needn't handle non-finite values.
Results may differ from the reference program's by a relative error of at most 0.0085.
Values may be sent and summed in bfloat16 or wider, within the bound.
A program may use at most 64 MiB of HBM per device.

```python
import jax
import jax.numpy as jnp
from jax import lax

NB = 1376
RMAX = 224
TILE_ROWS = 32
TILE_COLS = 32


def panel_ranks(key, salt, count):
    folded = jax.random.fold_in(key, salt)
    key_rank, key_spot = jax.random.split(folded)
    ranks = jax.random.randint(key_rank, (count,), RMAX // 4, RMAX + 1, dtype=jnp.int32)
    forced = jax.random.randint(key_spot, (), 0, count, dtype=jnp.int32)
    return jnp.where(jnp.arange(count, dtype=jnp.int32) == forced, RMAX, ranks).astype(jnp.int32)


def rank_pair(key):
    folded = jax.random.fold_in(key, 11)
    key_old, key_spot, key_new = jax.random.split(folded, 3)
    cells = TILE_ROWS * TILE_COLS
    old_ranks = jax.random.randint(key_old, (cells,), RMAX // 4, RMAX + 1, dtype=jnp.int32)
    forced_cell = jax.random.randint(key_spot, (), 0, cells, dtype=jnp.int32)
    old_ranks = jnp.where(jnp.arange(cells, dtype=jnp.int32) == forced_cell, RMAX, old_ranks)
    lower_end = old_ranks // 4
    upper_end = old_ranks // 2
    offsets = jax.random.randint(key_new, (cells,), 0, 1 << 20, dtype=jnp.int32)
    new_ranks = lower_end + offsets % (upper_end - lower_end + 1)
    new_ranks = jnp.where(old_ranks == RMAX, upper_end, new_ranks)
    return (old_ranks.reshape(TILE_ROWS, TILE_COLS).astype(jnp.int32), new_ranks.reshape(TILE_ROWS, TILE_COLS).astype(jnp.int32))


def draw_row_rank(key, part):
    return panel_ranks(key, 13, TILE_ROWS)


def draw_col_rank(key, part):
    return panel_ranks(key, 29, TILE_COLS)


def draw_old_rank(key, part):
    return rank_pair(key)[0]


def draw_new_rank(key, part):
    return rank_pair(key)[1]


def draw_diag_inverse(key, part):
    key_off, key_diag = jax.random.split(jax.random.fold_in(key, 17))
    spread = 0.5 / jnp.sqrt(jnp.float32(NB))
    raw = jnp.clip(jax.random.normal(key_off, (NB, NB), jnp.float32), -3.5, 3.5) * spread
    diagonal = jax.random.uniform(key_diag, (NB,), jnp.float32, 0.3, 0.45)
    lower = jnp.tril(raw, -1)
    return (lower + jnp.diag(diagonal)).astype(jnp.bfloat16)


def level_of(own_key, dims, cuts, low, top_value):
    def one(axis_at, parts):
        draws = jax.random.uniform(jax.random.fold_in(jax.random.fold_in(own_key, 6), axis_at), (parts,), jnp.float32, low / len(cuts), top_value / len(cuts))
        return jnp.repeat(jnp.exp(draws), dims[axis_at] // parts).reshape((-1,) + (1,) * (len(dims) - axis_at - 1))

    factor_of = one(*cuts[0])
    for cut in cuts[1:]:
        factor_of = factor_of * one(*cut)
    return factor_of


def scatter_about(key, extent, width, limit, cuts=(), kind=jnp.bfloat16):
    level = level_of(key, extent, cuts, -0.22, 0.18) if cuts else 1.0
    values = jax.random.normal(key, extent, jnp.float32) * width * level
    return jnp.minimum(jnp.maximum(values, -limit), limit).astype(kind)


def setup_inputs(seed: int = 0) -> dict:
    splits = jax.random.split(jax.random.key(seed), 13)
    return {
        "diag_inverse": draw_diag_inverse(jax.random.fold_in(splits[12], 71), 0),
        "row_u": scatter_about(splits[1], (TILE_ROWS, NB, RMAX), 1.0, 6.0, ((0, 32), (2, 32))),
        "row_v": scatter_about(splits[2], (TILE_ROWS, NB, RMAX), 0.1, 0.59765625, ((0, 32), (2, 32))),
        "col_u": scatter_about(splits[3], (TILE_COLS, NB, RMAX), 1.0, 6.0, ((0, 32), (2, 32))),
        "col_v": scatter_about(splits[4], (TILE_COLS, NB, RMAX), 0.1, 0.59765625, ((0, 32), (2, 32))),
        "tile_u": scatter_about(splits[5], (TILE_ROWS, TILE_COLS, NB, RMAX), 1.0, 6.0, ((0, 32), (1, 32))),
        "tile_v": scatter_about(splits[6], (TILE_ROWS, TILE_COLS, NB, RMAX), 1.0, 6.0, ((0, 32), (1, 32))),
        "sketch": scatter_about(splits[7], (NB, RMAX), 1.0, 6.0),
        "row_rank": draw_row_rank(jax.random.fold_in(splits[12], 71), 0),
        "col_rank": draw_col_rank(jax.random.fold_in(splits[12], 71), 0),
        "old_rank": draw_old_rank(jax.random.fold_in(splits[12], 71), 0),
        "new_rank": draw_new_rank(jax.random.fold_in(splits[12], 71), 0),
    }


precise_mode = lax.Precision.HIGHEST

def keep_mask(rank_cap, count):
    return jnp.arange(rank_cap, dtype=jnp.int32) < count

def solve_panel(inverse, right_side, counts):
    tile_count, row_count, rank_cap = right_side.shape
    keep_cols = jnp.arange(rank_cap, dtype=jnp.int32)[None, None, :] < counts[:, None, None]
    values = jnp.where(keep_cols, right_side, jnp.zeros_like(right_side))
    stacked = jnp.transpose(values, (1, 0, 2)).reshape(row_count, tile_count * rank_cap)
    solved = jnp.dot(inverse.astype(jnp.float32), stacked.astype(jnp.float32), preferred_element_type=jnp.float32)
    return jnp.transpose(solved.reshape(row_count, tile_count, rank_cap), (1, 0, 2)).astype(jnp.bfloat16)

def tile_update(base_u, base_v, left_u, left_w, right_u, right_w, sketch, old_count, new_count):
    row_count, rank_cap = base_u.shape
    kept_v = jnp.where(keep_mask(rank_cap, old_count)[None, :], base_v, jnp.zeros_like(base_v))
    new_keep = keep_mask(rank_cap, new_count)
    probe_cols = jnp.where(new_keep[None, :], sketch, jnp.zeros_like(sketch))
    core_mat = jnp.dot(left_w.T.astype(jnp.float32), right_w.astype(jnp.float32), preferred_element_type=jnp.float32).astype(jnp.bfloat16)
    left_small = jnp.dot(kept_v.T.astype(jnp.float32), probe_cols.astype(jnp.float32), preferred_element_type=jnp.float32).astype(jnp.bfloat16)
    across = jnp.dot(right_u.T.astype(jnp.float32), probe_cols.astype(jnp.float32), preferred_element_type=jnp.float32).astype(jnp.bfloat16)
    middle = jnp.dot(core_mat.astype(jnp.float32), across.astype(jnp.float32), preferred_element_type=jnp.float32).astype(jnp.bfloat16)
    range_y = jnp.dot(base_u.astype(jnp.float32), left_small.astype(jnp.float32), preferred_element_type=jnp.float32) - jnp.dot(left_u.astype(jnp.float32), middle.astype(jnp.float32), preferred_element_type=jnp.float32)
    padding = jnp.where(new_keep, 0.0, 1.0).astype(jnp.float32)
    gram = jnp.dot(range_y.T.astype(jnp.float32), range_y.astype(jnp.float32), precision=precise_mode, preferred_element_type=jnp.float32) + jnp.diag(padding)
    gram_factor = jnp.linalg.cholesky(gram)
    range_basis = jax.scipy.linalg.solve_triangular(gram_factor, range_y.T, lower=True).T
    new_u = (jnp.sqrt(jnp.float32(row_count)) * range_basis).astype(jnp.bfloat16)
    back_small = jnp.dot(base_u.T.astype(jnp.float32), new_u.astype(jnp.float32), preferred_element_type=jnp.float32).astype(jnp.bfloat16)
    side_small = jnp.dot(left_u.T.astype(jnp.float32), new_u.astype(jnp.float32), preferred_element_type=jnp.float32).astype(jnp.bfloat16)
    turned = jnp.dot(core_mat.T.astype(jnp.float32), side_small.astype(jnp.float32), preferred_element_type=jnp.float32).astype(jnp.bfloat16)
    summed = jnp.dot(kept_v.astype(jnp.float32), back_small.astype(jnp.float32), preferred_element_type=jnp.float32) - jnp.dot(right_u.astype(jnp.float32), turned.astype(jnp.float32), preferred_element_type=jnp.float32)
    new_v = (summed / jnp.float32(row_count)).astype(jnp.bfloat16)
    return (new_u, new_v)

def reference(diag_inverse, row_u, row_v, col_u, col_v, tile_u, tile_v, sketch, row_rank, col_rank, old_rank, new_rank):
    row_solved = solve_panel(diag_inverse, row_v, row_rank)
    col_solved = solve_panel(diag_inverse, col_v, col_rank)
    col_indices = jnp.arange(TILE_COLS, dtype=jnp.int32)

    def one_row(row_index):

        def one_tile(col_index):
            return tile_update(tile_u[row_index, col_index], tile_v[row_index, col_index], row_u[row_index], row_solved[row_index], col_u[col_index], col_solved[col_index], sketch, old_rank[row_index, col_index], new_rank[row_index, col_index])
        return lax.map(one_tile, col_indices)
    new_u, new_v = lax.map(one_row, jnp.arange(TILE_ROWS, dtype=jnp.int32))
    return (new_u, new_v)
```

```python
import jax
import jax.numpy as jnp
from jax import lax
from jax.experimental import pallas as pl
from jax.experimental.pallas import tpu as pltpu
from jax.sharding import PartitionSpec as P

NB = 1376
RANK = 224
HALF = 128
ROWS = 48
PANELS = 14
LANES = (384, 768, 1152, 1376)
HIGH = lax.Precision.HIGHEST
MESH_ID = pl.DeviceIdType.MESH
VMEM_LIMIT = 56 * 1024 * 1024


def dot_nt(a, b, **kw):
    return lax.dot_general(a, b, (((1,), (1,)), ((), ())), preferred_element_type=jnp.float32, **kw)


def dot_nn(a, b, **kw):
    return lax.dot_general(a, b, (((1,), (0,)), ((), ())), preferred_element_type=jnp.float32, **kw)


def prepare_kernel(row_rank, col_rank, diag, ru, rv, cu, cv, rs, cs, ds):
    col = lax.axis_index("col")
    row = lax.axis_index("row")
    zero_row = jnp.zeros((1, NB), jnp.bfloat16)
    spot = lax.broadcasted_iota(jnp.int32, (7, NB), 0)
    for u, v, out, first, count in ((ru, rv, rs, 7 * col, row_rank[0]), (cu, cv, cs, 7 * row, col_rank[0])):
        out[0, 0:7, :] = u[...]
        out[0, 7:8, :] = zero_row
        kept = jnp.where(spot + first < count, v[...].astype(jnp.float32), 0.0)
        out[1, 0:7, :] = kept.astype(jnp.bfloat16)
        out[1, 7:8, :] = zero_row
    ds[0:43, :] = diag[...]
    ds[43:48, :] = jnp.zeros((5, NB), jnp.bfloat16)


def prepare(row_rank, col_rank, diag, ru, rv, cu, cv):
    vmem = pl.BlockSpec(memory_space=pltpu.VMEM)
    return pl.pallas_call(
        prepare_kernel,
        name="prepare",
        in_specs=[pl.BlockSpec(memory_space=pltpu.SMEM)] * 2 + [vmem] * 5,
        out_specs=[vmem] * 3,
        out_shape=[
            jax.ShapeDtypeStruct((2, 8, NB), jnp.bfloat16),
            jax.ShapeDtypeStruct((2, 8, NB), jnp.bfloat16),
            jax.ShapeDtypeStruct((ROWS, NB), jnp.bfloat16),
        ],
    )(row_rank, col_rank, diag, ru, rv, cu, cv)


def gather_kernel(rs, cs, ds, r_all, c_all, d_all, own, quad_s, quad_r, zs, zr, ys, yr, xs, xr,
                  dys, dyr, dxs, dxr, ps, pr):
    row, col = lax.axis_index("row"), lax.axis_index("col")
    x, yh = row // 4, row % 4
    z, q = col // 4, col % 4
    core = col % 2

    def mate(k):
        low = jnp.where(k % 2 == 1, 1 - q % 2, q % 2)
        high = jnp.where(k // 2 == 1, 1 - q // 2, q // 2)
        return (row, z * 4 + high * 2 + low)

    def along_z(step):
        return (row, ((z + step) % 8) * 4 + q)

    def along_y(step):
        return (x * 4 + (yh + step) % 4, col)

    def along_x(step):
        return (((x + step) % 8) * 4 + yh, col)

    def remote(src, send, recv, device):
        return pltpu.make_async_remote_copy(
            src_ref=src, dst_ref=src, send_sem=send, recv_sem=recv, device_id=device, device_id_type=MESH_ID
        )

    partners = (
        [mate(1), mate(2), mate(3), along_z(1), along_z(7)]
        + [along_y(1), along_y(2), along_y(3), along_x(1), along_x(7)]
    )
    barrier = pltpu.get_barrier_semaphore()
    for device in partners:
        pl.semaphore_signal(barrier, inc=1, device_id=device, device_id_type=MESH_ID)
    local = [
        pltpu.make_async_copy(cs, c_all.at[x, yh], own.at[0]),
        pltpu.make_async_copy(ds, d_all.at[x, yh], own.at[1]),
        pltpu.make_async_copy(rs, r_all.at[z, q], own.at[2]),
    ]
    for copy in local:
        copy.start()
    pl.semaphore_wait(barrier, len(partners))
    for copy in local:
        copy.wait()

    sent = []

    def go(copy):
        copy.start()
        sent.append(copy.wait_send)

    for t in (1, 2, 3):
        go(remote(c_all.at[x, yh], ys.at[t], yr.at[t], along_y(t)))

    @pl.when(yh // 2 == core)
    def _():
        for t in (1, 2, 3):
            remote(d_all.at[x, yh], dys.at[t], dyr.at[yh % 2], along_y(t)).start()

    def sent_d():
        @pl.when(yh // 2 == core)
        def _():
            for t in (1, 2, 3):
                remote(d_all.at[x, yh], dys.at[t], dyr.at[yh % 2], along_y(t)).wait_send()

    sent.append(sent_d)
    for k in (1, 2, 3):
        go(remote(r_all.at[z, q], quad_s.at[k], quad_r.at[k], mate(k)))

    def by_class(xo, act):
        for k, lanes in enumerate(LANES):
            @pl.when(xo // 2 == k)
            def _(lanes=lanes):
                act(lanes)

    def ring_length(way, part, parts):
        return 4 if (part < parts // 2) == (way == 0) else 3

    def z_copy(way, step, k):
        zo = (z + (8 - step if way == 0 else step)) % 8
        slot = mate(k)[1] % 4
        return remote(r_all.at[zo, slot], zs.at[way, step, k], zr.at[way, step, k], along_z(1 if way == 0 else 7))

    def x_copy(way, step, t):
        xo = (x + (8 - step if way == 0 else step)) % 8
        return remote(
            c_all.at[xo, (yh + 4 - t) % 4], xs.at[way, step, t], xr.at[way, step, t], along_x(1 if way == 0 else 7)
        )

    def dx_do(way, step, b, method):
        xo = (x + (8 - step if way == 0 else step)) % 8

        def act(lanes):
            copy = remote(
                d_all.at[xo, 2 * core + b, :, pl.ds(0, lanes)],
                dxs.at[way, step, b], dxr.at[way, step, b], along_x(1 if way == 0 else 7),
            )
            getattr(copy, method)()

        by_class(xo, act)

    def share_do(way, step, b, method):
        xo = (x + (8 - step if way == 0 else step)) % 8
        theirs = method == "wait_recv"
        block = 2 * (1 - core if theirs else core) + b
        index = step if way == 0 else 4 + step

        def act(lanes):
            copy = remote(d_all.at[xo, block, :, pl.ds(0, lanes)], ps.at[index, b], pr.at[index, b], mate(1))
            getattr(copy, method)()

        if step == 0:
            @pl.when(block != yh)
            def _():
                by_class(xo, act)
        else:
            by_class(xo, act)

    def arrive_z(way, step, k):
        zo = (z + (8 - step if way == 0 else step)) % 8
        slot = mate(k)[1] % 4
        remote(r_all.at[zo, slot], zs.at[way, step - 1, k], zr.at[way, step - 1, k], along_z(1)).wait_recv()

    def arrive_x(way, step, t):
        xo = (x + (8 - step if way == 0 else step)) % 8
        remote(
            c_all.at[xo, (yh + 4 - t) % 4], xs.at[way, step - 1, t], xr.at[way, step - 1, t], along_x(1)
        ).wait_recv()

    def arrive_dx(way, step, b):
        xo = (x + (8 - step if way == 0 else step)) % 8

        def act(lanes):
            remote(
                d_all.at[xo, 2 * core + b, :, pl.ds(0, lanes)],
                dxs.at[way, step - 1, b], dxr.at[way, step - 1, b], along_x(1),
            ).wait_recv()

        by_class(xo, act)

    for step in range(5):
        for k in range(4):
            if step == 0 and k > 0:
                remote(r_all.at[z, mate(k)[1] % 4], quad_s.at[k], quad_r.at[k], mate(k)).wait_recv()
            for way in (0, 1):
                length = ring_length(way, k, 4)
                if 1 <= step <= length:
                    arrive_z(way, step, k)
                if step < length:
                    go(z_copy(way, step, k))
        for t in range(4):
            if step == 0 and t > 0:
                remote(c_all.at[x, (yh + 4 - t) % 4], ys.at[t], yr.at[t], along_y(t)).wait_recv()
            for way in (0, 1):
                length = ring_length(way, t, 4)
                if 1 <= step <= length:
                    arrive_x(way, step, t)
                if step < length:
                    go(x_copy(way, step, t))
            if t % 2 == 0:
                continue
            b = t // 2
            if step == 0:
                @pl.when(2 * core + b != yh)
                def _(b=b):
                    remote(d_all.at[x, 2 * core + b], dys.at[1], dyr.at[b], along_y(1)).wait_recv()
            for way in (0, 1):
                length = ring_length(way, b, 2)
                if 1 <= step <= length:
                    arrive_dx(way, step, b)
                if step < length:
                    dx_do(way, step, b, "start")
                    sent.append(lambda way=way, step=step, b=b: dx_do(way, step, b, "wait_send"))
                if (step == 0 and way == 0) or 1 <= step <= length:
                    share_do(way, step, b, "start")
                    sent.append(lambda way=way, step=step, b=b: share_do(way, step, b, "wait_send"))
    for b in (0, 1):
        for way in (0, 1):
            for step in range(ring_length(way, b, 2) + 1):
                if step > 0 or way == 0:
                    share_do(way, step, b, "wait_recv")
    for wait in sent:
        wait()


def gather(rs, cs, ds):
    dma = pltpu.SemaphoreType.DMA
    anywhere = pl.BlockSpec(memory_space=pl.ANY)
    return pl.pallas_call(
        gather_kernel,
        name="gather",
        in_specs=[anywhere] * 3,
        out_specs=[anywhere] * 3,
        out_shape=[
            jax.ShapeDtypeStruct((8, 4, 2, 8, NB), jnp.bfloat16),
            jax.ShapeDtypeStruct((8, 4, 2, 8, NB), jnp.bfloat16),
            jax.ShapeDtypeStruct((8, 4, ROWS, NB), jnp.bfloat16),
        ],
        scratch_shapes=[
            dma((3,)), dma((4,)), dma((4,)), dma((2, 4, 4)), dma((2, 4, 4)), dma((4,)), dma((4,)),
            dma((2, 4, 4)), dma((2, 4, 4)), dma((4,)), dma((2,)), dma((2, 4, 2)), dma((2, 4, 2)),
            dma((9, 2)), dma((9, 2)),
        ],
        compiler_params=pltpu.CompilerParams(collective_id=0, has_side_effects=True),
    )(rs, cs, ds)


def inverse_factor(gram):
    a = [gram[8 * i : 8 * i + 8, :] for i in range(PANELS)]
    lane = lax.broadcasted_iota(jnp.int32, (8, HALF), 1)
    line = lax.broadcasted_iota(jnp.int32, (8, HALF), 0)
    w = [jnp.where(lane == line + 8 * i, 1.0, 0.0).astype(jnp.float32) for i in range(PANELS)]
    done = []
    for k in range(PANELS):
        at = 8 * k
        d = [[jnp.broadcast_to(a[k][i : i + 1, at + j : at + j + 1], (8, HALF)) for j in range(i + 1)] for i in range(8)]
        low = [[None] * 8 for _ in range(8)]
        inv = []
        for j in range(8):
            inv.append(lax.rsqrt(d[j][j]))
            for i in range(j + 1, 8):
                low[i][j] = d[i][j] * inv[j]
            for i in range(j + 1, 8):
                for m in range(j + 1, i + 1):
                    d[i][m] = d[i][m] - low[i][j] * low[m][j]
        rows_a = [jnp.broadcast_to(a[k][i : i + 1, :], (8, HALF)) for i in range(8)]
        rows_w = [jnp.broadcast_to(w[k][i : i + 1, :], (8, HALF)) for i in range(8)]
        for j in range(8):
            rows_a[j] = rows_a[j] * inv[j]
            rows_w[j] = rows_w[j] * inv[j]
            for i in range(j + 1, 8):
                rows_a[i] = rows_a[i] - low[i][j] * rows_a[j]
                rows_w[i] = rows_w[i] - low[i][j] * rows_w[j]
        for i in range(k + 1, PANELS):
            cols = [jnp.broadcast_to(a[i][:, at + j : at + j + 1], (8, HALF)) for j in range(8)]
            for j in range(8):
                cols[j] = cols[j] * inv[j]
                for m in range(j + 1, 8):
                    cols[m] = cols[m] - cols[j] * low[m][j]
                a[i] = a[i] - cols[j] * rows_a[j]
                w[i] = w[i] - cols[j] * rows_w[j]
        final = rows_w[0]
        for j in range(1, 8):
            final = jnp.where(line == j, rows_w[j], final)
        done.append(final)
    done.append(jnp.zeros((HALF - 8 * PANELS, HALF), jnp.float32))
    return jnp.concatenate(done, axis=0)


def update_kernel(old_rank, new_rank, r_all, c_all, d_all, tu, tv, sk, new_u, new_v, solved, range_y):
    bf = jnp.bfloat16
    f32 = jnp.float32
    old_count, new_count = old_rank[0, 0], new_rank[0, 0]
    ru = r_all[:, 0].reshape(256, NB)
    rv = r_all[:, 1].reshape(256, NB)
    cu = c_all[:, 0].reshape(256, NB)
    cv = c_all[:, 1].reshape(256, NB)
    new_line = lax.broadcasted_iota(jnp.int32, (HALF, NB), 0)
    probe = jnp.where(new_line < new_count, sk[0:HALF, :].astype(f32), 0.0).astype(bf)
    old_keep = lax.broadcasted_iota(jnp.int32, (HALF, RANK), 1) < old_count
    left_small = jnp.where(old_keep, dot_nt(probe, tv[...]), 0.0).astype(bf)
    across = dot_nt(probe, cu).astype(bf)
    base = dot_nn(left_small, tu[...])
    vs = jnp.concatenate([rv, cv], axis=0)
    for xo in range(8):
        lanes = LANES[xo // 2]
        block = d_all[xo, :, :, 0:lanes].reshape(4 * ROWS, lanes)
        solved[:, pl.ds(4 * ROWS * xo, 4 * ROWS)] = dot_nt(vs[:, 0:lanes], block).astype(bf)
    core = dot_nt(solved[0:256, :], solved[256:512, :]).astype(bf)
    middle = dot_nt(across, core).astype(bf)
    y = base - dot_nn(middle, ru)
    range_y[...] = y
    gram = dot_nt(y, y, precision=HIGH)
    lane = lax.broadcasted_iota(jnp.int32, (HALF, HALF), 1)
    line = lax.broadcasted_iota(jnp.int32, (HALF, HALF), 0)
    gram = gram + jnp.where((lane == line) & (line >= new_count), 1.0, 0.0)
    inverse = inverse_factor(gram)
    u = (jnp.sqrt(f32(NB)) * dot_nn(inverse, range_y[...], precision=HIGH)).astype(bf)
    new_u[0:HALF, :] = u
    new_u[HALF:RANK, :] = jnp.zeros((RANK - HALF, NB), bf)
    back = jnp.where(old_keep, dot_nt(u, tu[...]), 0.0).astype(bf)
    side = dot_nt(u, ru).astype(bf)
    turned = dot_nn(side, core).astype(bf)
    new_v[0:HALF, :] = ((dot_nn(back, tv[...]) - dot_nn(turned, cu)) / f32(NB)).astype(bf)
    new_v[HALF:RANK, :] = jnp.zeros((RANK - HALF, NB), bf)


def update(old_rank, new_rank, r_all, c_all, d_all, tu, tv, sk):
    vmem = pl.BlockSpec(memory_space=pltpu.VMEM)
    out = jax.ShapeDtypeStruct((RANK, NB), jnp.bfloat16)
    return pl.pallas_call(
        update_kernel,
        name="update",
        in_specs=[pl.BlockSpec(memory_space=pltpu.SMEM)] * 2 + [vmem] * 6,
        out_specs=[vmem] * 2,
        out_shape=[out, out],
        scratch_shapes=[pltpu.VMEM((512, 32 * ROWS), jnp.bfloat16), pltpu.VMEM((HALF, NB), jnp.float32)],
        compiler_params=pltpu.CompilerParams(vmem_limit_bytes=VMEM_LIMIT),
    )(old_rank, new_rank, r_all.reshape(32, 2, 8, NB), c_all.reshape(32, 2, 8, NB), d_all, tu, tv, sk)


def on_device(diag_inverse, row_u, row_v, col_u, col_v, tile_u, tile_v, sketch, row_rank, col_rank, old_rank, new_rank):
    rs, cs, ds = prepare(row_rank, col_rank, diag_inverse, row_u[0].T, row_v[0].T, col_u[0].T, col_v[0].T)
    r_all, c_all, d_all = gather(rs, cs, ds)
    new_u, new_v = update(old_rank, new_rank, r_all, c_all, d_all, tile_u[0, 0].T, tile_v[0, 0].T, sketch.T)
    return (new_u.T[None, None], new_v.T[None, None])


def solution(mesh):
    in_specs = (
        P("row", None),
        P("row", None, "col"),
        P("row", None, "col"),
        P("col", None, "row"),
        P("col", None, "row"),
        P("row", "col", None, None),
        P("row", "col", None, None),
        P(),
        P("row"),
        P("col"),
        P("row", "col"),
        P("row", "col"),
    )
    out_specs = (P("row", "col", None, None), P("row", "col", None, None))
    return jax.shard_map(
        on_device, mesh=mesh, in_specs=in_specs, out_specs=out_specs, check_vma=False
    )
```

```python
import jax
import jax.numpy as jnp
from jax import lax
from jax.experimental import pallas as pl
from jax.experimental.pallas import tpu as pltpu
from jax.sharding import PartitionSpec as P

NB = 1376
RANK = 224
HALF = 128
ROWS = 48
PANELS = 14
LANES = (384, 768, 1152, 1376)
HIGH = lax.Precision.HIGHEST
MESH_ID = pl.DeviceIdType.MESH
VMEM_LIMIT = 56 * 1024 * 1024


def dot_nt(a, b, **kw):
    return lax.dot_general(a, b, (((1,), (1,)), ((), ())), preferred_element_type=jnp.float32, **kw)


def dot_nn(a, b, **kw):
    return lax.dot_general(a, b, (((1,), (0,)), ((), ())), preferred_element_type=jnp.float32, **kw)


def prepare_kernel(row_rank, col_rank, diag, ru, rv, cu, cv, rs, cs, ds):
    col = lax.axis_index("col")
    row = lax.axis_index("row")
    zero_row = jnp.zeros((1, NB), jnp.bfloat16)
    spot = lax.broadcasted_iota(jnp.int32, (7, NB), 0)
    for u, v, out, first, count in ((ru, rv, rs, 7 * col, row_rank[0]), (cu, cv, cs, 7 * row, col_rank[0])):
        out[0, 0:7, :] = u[...]
        out[0, 7:8, :] = zero_row
        kept = jnp.where(spot + first < count, v[...].astype(jnp.float32), 0.0)
        out[1, 0:7, :] = kept.astype(jnp.bfloat16)
        out[1, 7:8, :] = zero_row
    ds[0:43, :] = diag[...]
    ds[43:48, :] = jnp.zeros((5, NB), jnp.bfloat16)


def prepare(row_rank, col_rank, diag, ru, rv, cu, cv):
    vmem = pl.BlockSpec(memory_space=pltpu.VMEM)
    return pl.pallas_call(
        prepare_kernel,
        name="prepare",
        in_specs=[pl.BlockSpec(memory_space=pltpu.SMEM)] * 2 + [vmem] * 5,
        out_specs=[vmem] * 3,
        out_shape=[
            jax.ShapeDtypeStruct((2, 8, NB), jnp.bfloat16),
            jax.ShapeDtypeStruct((2, 8, NB), jnp.bfloat16),
            jax.ShapeDtypeStruct((ROWS, NB), jnp.bfloat16),
        ],
    )(row_rank, col_rank, diag, ru, rv, cu, cv)


def gather_kernel(rs, cs, ds, r_all, c_all, d_all, own, quad_s, quad_r, zs, zr, zps, zpr, ys, yr, xs, xr,
                  dxs, dxr, dfs, dfr, dhs, dhr, dbs, ps, pr):
    row, col = lax.axis_index("row"), lax.axis_index("col")
    x, yh = row // 4, row % 4
    z, q = col // 4, col % 4
    low, core = q // 2, q % 2

    def quad(k):
        there = jnp.where(k % 2 == 1, 1 - core, core)
        return jnp.where(k // 2 == 1, 1 - low, low) * 2 + there

    def mate(k):
        return (row, z * 4 + quad(k))

    def along_z(step):
        return (row, (z + step) % 8 * 4 + q)

    def along_y(step):
        return (x * 4 + (yh + step) % 4, col)

    def along_x(step):
        return ((x + step) % 8 * 4 + yh, col)

    def beside(way):
        there = yh + low if way == 0 else yh + low + 3
        return (x * 4 + there % 4, z * 4 + (1 - low) * 2 + core)

    def remote(src, dst, send, recv, device):
        return pltpu.make_async_remote_copy(
            src_ref=src, dst_ref=dst, send_sem=send, recv_sem=recv, device_id=device, device_id_type=MESH_ID
        )

    across_pair = (x * 4 + (yh + 2 * low + 3) % 4, z * 4 + (1 - low) * 2 + core)
    partners = (
        [mate(1), mate(2), mate(3), along_z(1), along_z(7), across_pair]
        + [along_y(1), along_y(2), along_y(3), along_x(1), along_x(2), along_x(6), along_x(7)]
    )
    barrier = pltpu.get_barrier_semaphore()
    for device in partners:
        pl.semaphore_signal(barrier, inc=1, device_id=device, device_id_type=MESH_ID)
    local = [
        pltpu.make_async_copy(cs, c_all.at[x, yh], own.at[0]),
        pltpu.make_async_copy(ds, d_all.at[x, yh], own.at[1]),
        pltpu.make_async_copy(rs, r_all.at[z, q], own.at[2]),
    ]
    for copy in local:
        copy.start()
    pl.semaphore_wait(barrier, len(partners))

    ends = []

    def go(copy):
        copy.start()
        ends.append(copy.wait_send)

    def by_class(xo, act):
        for k, lanes in enumerate(LANES):
            @pl.when(xo // 2 == k)
            def _(lanes=lanes):
                act(lanes)

    def origin(here, way, step):
        return (here + (8 - step if way == 0 else step)) % 8

    def z_length(way, k):
        return 4 if (k == 0) == (way == 0) else 3

    def z_copy(way, step, k):
        slot = r_all.at[origin(z, way, step), quad(k)]
        src = rs if step == 0 and k == 0 else slot
        return remote(src, slot, zs.at[way, step, k // 2], zr.at[way, step, k // 2], along_z(1 if way == 0 else 7))

    def z_tick(step):
        for k in (0, 2):
            if step == 0 and k == 2:
                remote(rs, r_all.at[z, quad(2)], quad_s.at[2], quad_r.at[2], mate(2)).wait_recv()
            for way in (0, 1):
                if 1 <= step <= z_length(way, k):
                    slot = r_all.at[origin(z, way, step), quad(k)]
                    remote(slot, slot, zs.at[way, step - 1, k // 2], zr.at[way, step - 1, k // 2], mate(1)).wait_recv()
                if step < z_length(way, k):
                    go(z_copy(way, step, k))
                if 1 <= step <= z_length(way, k):
                    sems = (zps.at[way, step - 1, k // 2], zpr.at[way, step - 1, k // 2])
                    go(remote(slot, slot, *sems, mate(1)))
                    theirs = r_all.at[origin(z, way, step), quad(k + 1)]
                    ends.append(remote(theirs, theirs, *sems, mate(1)).wait_recv)

    def x_length(way, t):
        return 4 if (t % 2 == 1) == (way == 0) else 3

    def x_tick(t, step):
        if step == 0 and t > 0:
            remote(cs, c_all.at[x, (yh + 4 - t) % 4], ys.at[t], yr.at[t], along_y(t)).wait_recv()
        for way in (0, 1):
            slot = c_all.at[origin(x, way, step), (yh + 4 - t) % 4]
            ahead = along_x(1 if way == 0 else 7)
            if 1 <= step <= x_length(way, t):
                remote(slot, slot, xs.at[way, step - 1, t], xr.at[way, step - 1, t], ahead).wait_recv()
            if step < x_length(way, t):
                src = cs if step == 0 and t == 0 else slot
                go(remote(src, slot, xs.at[way, step, t], xr.at[way, step, t], ahead))

    chunks = [(0, 0), (0, 1), (1, 1), (0, 2), (1, 2), (0, 3), (1, 3), (0, 4)]

    def d_part(xo, there, half, lanes):
        return d_all.at[xo, there % 4, half, :, pl.ds(0, lanes)]

    def d_run(method, j, there, send, recv, device, mine=False):
        xo = origin(x, *chunks[j])

        def act(lanes):
            part = d_part(xo, there, core, lanes)
            src = ds.at[core, :, pl.ds(0, lanes)] if mine else part
            getattr(remote(src, part, send, recv, device), method)()

        by_class(xo, act)

    def d_send(*args, when=None, **kw):
        if when is None:
            d_run("start", *args, **kw)
            ends.append(lambda: d_run("wait_send", *args, **kw))
        else:
            guarded(low == when, lambda: d_run("start", *args, **kw))
            ends.append(lambda: guarded(low == when, lambda: d_run("wait_send", *args, **kw)))

    def d_wait(j, there, half, send, recv):
        xo = origin(x, *chunks[j])

        def act(lanes):
            part = d_part(xo, there, half, lanes)
            remote(part, part, send, recv, mate(1)).wait_recv()

        by_class(xo, act)

    def share(j, there, index):
        sems = (ps.at[index, j], pr.at[index, j])
        d_send(j, there, *sems, mate(1))
        ends.append(lambda: d_wait(j, there, 1 - core, *sems))

    def guarded(condition, act):
        @pl.when(condition)
        def _():
            act()

    def y_send(way, j, full, when):
        base = yh + low + 3 if way == 0 else yh + low
        if full:
            mine = j == 0 and when == 1 - way
            d_send(j, base, dfs.at[way, j], dfr.at[way, j], beside(way), when=when, mine=mine)
        else:
            there = base + 3 if way == 0 else base + 1
            beyond = along_y(1 if way == 0 else 3)
            d_send(j, there, dbs.at[way, j], dhr.at[way, j], beyond, when=when)
            d_send(j, there, dhs.at[way, j], dhr.at[way, j], beside(way), when=when)

    def late_share(j, there, index, when):
        sems = (ps.at[index, j], pr.at[index, j])
        d_send(j, there, *sems, mate(1), when=when)
        ends.append(lambda: guarded(low == when, lambda: d_wait(j, there, 1 - core, *sems)))

    reached = [0, 1, 1, 1, 1, 2, 2, 2]

    def y_tick(tick):
        order = sorted(range(8), key=lambda j: reached[j])
        for hop in (0, 1, 2, 3):
            for j in order:
                if tick - reached[j] != hop:
                    continue
                for way in (0, 1):
                    first = 1 - way
                    half = j % 2 == way
                    beside_pair = yh + 3 if way == 0 else yh + 1
                    if hop == 0:
                        y_send(way, j, True, first)
                    elif hop in (1, 2):
                        here = 1 - first if hop == 1 else first
                        guarded(
                            low == here,
                            lambda: d_wait(j, beside_pair, core, dfs.at[way, j], dfr.at[way, j]),
                        )
                        if hop == 1:
                            y_send(way, j, True, here)
                        elif half:
                            y_send(way, j, False, here)
                        late_share(j, beside_pair, 1 + way, here)
                    elif half:
                        d_wait(j, yh + 2, core, dhs.at[way, j], dhr.at[way, j])
                        share(j, yh + 2, 3)

    def dx_send(way, far, step, mine):
        j = 0 if mine else chunks.index((way, 2))
        d_send(
            j, yh, dxs.at[way, far - 1], dxr.at[way, far - 1], along_x(step if way == 0 else 8 - step), mine=mine
        )

    def dx_wait(way, far):
        d_wait(chunks.index((way, far)), yh, core, dxs.at[way, far - 1], dxr.at[way, far - 1])

    def dx_tick(tick):
        if tick == 0:
            for way in (0, 1):
                dx_send(way, 2, 2, True)
            for way in (0, 1):
                dx_send(way, 1, 1, True)
        if tick == 1:
            dx_wait(0, 2)
            dx_send(0, 4, 2, False)
            dx_send(0, 3, 1, False)
            dx_wait(1, 2)
            dx_send(1, 3, 1, False)
            for way in (0, 1):
                dx_wait(way, 1)
        if tick == 2:
            for way in (0, 1):
                dx_wait(way, 3)
            dx_wait(0, 4)
        for j in range(1, 8):
            if reached[j] == tick:
                share(j, yh, 0)

    for t in (1, 2, 3):
        go(remote(cs, c_all.at[x, yh], ys.at[t], yr.at[t], along_y(t)))
    for k in (2, 1, 3):
        copy = remote(rs, r_all.at[z, q], quad_s.at[k], quad_r.at[k], mate(k))
        go(copy)
        if k != 2:
            theirs = r_all.at[z, quad(k)]
            ends.append(remote(theirs, theirs, quad_s.at[k], quad_r.at[k], mate(k)).wait_recv)
    for tick in range(6):
        if tick <= 2:
            dx_tick(tick)
        y_tick(tick)
        if tick <= 4:
            x_tick(0, tick)
            z_tick(tick)
        if tick >= 1:
            for t in (1, 3, 2):
                x_tick(t, tick - 1)
    for wait in ends:
        wait()
    for copy in local:
        copy.wait()


def gather(rs, cs, ds):
    dma = pltpu.SemaphoreType.DMA
    anywhere = pl.BlockSpec(memory_space=pl.ANY)
    return pl.pallas_call(
        gather_kernel,
        name="gather",
        in_specs=[anywhere] * 3,
        out_specs=[anywhere] * 3,
        out_shape=[
            jax.ShapeDtypeStruct((8, 4, 2, 8, NB), jnp.bfloat16),
            jax.ShapeDtypeStruct((8, 4, 2, 8, NB), jnp.bfloat16),
            jax.ShapeDtypeStruct((8, 4, 2, ROWS // 2, NB), jnp.bfloat16),
        ],
        scratch_shapes=[
            dma((3,)), dma((4,)), dma((4,)), dma((2, 4, 2)), dma((2, 4, 2)), dma((2, 4, 2)), dma((2, 4, 2)),
            dma((4,)), dma((4,)), dma((2, 4, 4)), dma((2, 4, 4)), dma((2, 4)), dma((2, 4)),
            dma((2, 8)), dma((2, 8)), dma((2, 8)), dma((2, 8)), dma((2, 8)), dma((4, 8)), dma((4, 8)),
        ],
        compiler_params=pltpu.CompilerParams(collective_id=0, has_side_effects=True),
    )(rs, cs, ds)


def inverse_factor(gram):
    a = [gram[8 * i : 8 * i + 8, :] for i in range(PANELS)]
    lane = lax.broadcasted_iota(jnp.int32, (8, HALF), 1)
    line = lax.broadcasted_iota(jnp.int32, (8, HALF), 0)
    w = [jnp.where(lane == line + 8 * i, 1.0, 0.0).astype(jnp.float32) for i in range(PANELS)]
    done = []
    for k in range(PANELS):
        at = 8 * k
        d = [[jnp.broadcast_to(a[k][i : i + 1, at + j : at + j + 1], (8, HALF)) for j in range(i + 1)] for i in range(8)]
        low = [[None] * 8 for _ in range(8)]
        inv = []
        for j in range(8):
            inv.append(lax.rsqrt(d[j][j]))
            for i in range(j + 1, 8):
                low[i][j] = d[i][j] * inv[j]
            for i in range(j + 1, 8):
                for m in range(j + 1, i + 1):
                    d[i][m] = d[i][m] - low[i][j] * low[m][j]
        rows_a = [jnp.broadcast_to(a[k][i : i + 1, :], (8, HALF)) for i in range(8)]
        rows_w = [jnp.broadcast_to(w[k][i : i + 1, :], (8, HALF)) for i in range(8)]
        for j in range(8):
            rows_a[j] = rows_a[j] * inv[j]
            rows_w[j] = rows_w[j] * inv[j]
            for i in range(j + 1, 8):
                rows_a[i] = rows_a[i] - low[i][j] * rows_a[j]
                rows_w[i] = rows_w[i] - low[i][j] * rows_w[j]
        for i in range(k + 1, PANELS):
            cols = [jnp.broadcast_to(a[i][:, at + j : at + j + 1], (8, HALF)) for j in range(8)]
            for j in range(8):
                cols[j] = cols[j] * inv[j]
                for m in range(j + 1, 8):
                    cols[m] = cols[m] - cols[j] * low[m][j]
                a[i] = a[i] - cols[j] * rows_a[j]
                w[i] = w[i] - cols[j] * rows_w[j]
        final = rows_w[0]
        for j in range(1, 8):
            final = jnp.where(line == j, rows_w[j], final)
        done.append(final)
    done.append(jnp.zeros((HALF - 8 * PANELS, HALF), jnp.float32))
    return jnp.concatenate(done, axis=0)


def update_kernel(old_rank, new_rank, r_all, c_all, d_all, tu, tv, sk, new_u, new_v, solved, range_y):
    bf = jnp.bfloat16
    f32 = jnp.float32
    old_count, new_count = old_rank[0, 0], new_rank[0, 0]
    ru = r_all[:, 0].reshape(256, NB)
    rv = r_all[:, 1].reshape(256, NB)
    cu = c_all[:, 0].reshape(256, NB)
    cv = c_all[:, 1].reshape(256, NB)
    new_line = lax.broadcasted_iota(jnp.int32, (HALF, NB), 0)
    probe = jnp.where(new_line < new_count, sk[0:HALF, :].astype(f32), 0.0).astype(bf)
    old_keep = lax.broadcasted_iota(jnp.int32, (HALF, RANK), 1) < old_count
    left_small = jnp.where(old_keep, dot_nt(probe, tv[...]), 0.0).astype(bf)
    across = dot_nt(probe, cu).astype(bf)
    base = dot_nn(left_small, tu[...])
    vs = jnp.concatenate([rv, cv], axis=0)
    for xo in range(8):
        lanes = LANES[xo // 2]
        block = d_all[xo, :, :, 0:lanes].reshape(4 * ROWS, lanes)
        solved[:, pl.ds(4 * ROWS * xo, 4 * ROWS)] = dot_nt(vs[:, 0:lanes], block).astype(bf)
    core = dot_nt(solved[0:256, :], solved[256:512, :]).astype(bf)
    middle = dot_nt(across, core).astype(bf)
    y = base - dot_nn(middle, ru)
    range_y[...] = y
    gram = dot_nt(y, y, precision=HIGH)
    lane = lax.broadcasted_iota(jnp.int32, (HALF, HALF), 1)
    line = lax.broadcasted_iota(jnp.int32, (HALF, HALF), 0)
    gram = gram + jnp.where((lane == line) & (line >= new_count), 1.0, 0.0)
    inverse = inverse_factor(gram)
    u = (jnp.sqrt(f32(NB)) * dot_nn(inverse, range_y[...], precision=HIGH)).astype(bf)
    new_u[0:HALF, :] = u
    new_u[HALF:RANK, :] = jnp.zeros((RANK - HALF, NB), bf)
    back = jnp.where(old_keep, dot_nt(u, tu[...]), 0.0).astype(bf)
    side = dot_nt(u, ru).astype(bf)
    turned = dot_nn(side, core).astype(bf)
    new_v[0:HALF, :] = ((dot_nn(back, tv[...]) - dot_nn(turned, cu)) / f32(NB)).astype(bf)
    new_v[HALF:RANK, :] = jnp.zeros((RANK - HALF, NB), bf)


def update(old_rank, new_rank, r_all, c_all, d_all, tu, tv, sk):
    vmem = pl.BlockSpec(memory_space=pltpu.VMEM)
    out = jax.ShapeDtypeStruct((RANK, NB), jnp.bfloat16)
    return pl.pallas_call(
        update_kernel,
        name="update",
        in_specs=[pl.BlockSpec(memory_space=pltpu.SMEM)] * 2 + [vmem] * 6,
        out_specs=[vmem] * 2,
        out_shape=[out, out],
        scratch_shapes=[pltpu.VMEM((512, 32 * ROWS), jnp.bfloat16), pltpu.VMEM((HALF, NB), jnp.float32)],
        compiler_params=pltpu.CompilerParams(vmem_limit_bytes=VMEM_LIMIT),
    )(old_rank, new_rank, r_all.reshape(32, 2, 8, NB), c_all.reshape(32, 2, 8, NB), d_all.reshape(8, 4, ROWS, NB), tu, tv, sk)


def on_device(diag_inverse, row_u, row_v, col_u, col_v, tile_u, tile_v, sketch, row_rank, col_rank, old_rank, new_rank):
    rs, cs, ds = prepare(row_rank, col_rank, diag_inverse, row_u[0].T, row_v[0].T, col_u[0].T, col_v[0].T)
    r_all, c_all, d_all = gather(rs, cs, ds.reshape(2, ROWS // 2, NB))
    new_u, new_v = update(old_rank, new_rank, r_all, c_all, d_all, tile_u[0, 0].T, tile_v[0, 0].T, sketch.T)
    return (new_u.T[None, None], new_v.T[None, None])


def solution(mesh):
    in_specs = (
        P("row", None),
        P("row", None, "col"),
        P("row", None, "col"),
        P("col", None, "row"),
        P("col", None, "row"),
        P("row", "col", None, None),
        P("row", "col", None, None),
        P(),
        P("row"),
        P("col"),
        P("row", "col"),
        P("row", "col"),
    )
    out_specs = (P("row", "col", None, None), P("row", "col", None, None))
    return jax.shard_map(
        on_device, mesh=mesh, in_specs=in_specs, out_specs=out_specs, check_vma=False
    )
```

```python
import jax
import jax.numpy as jnp
from jax import lax
from jax.experimental import pallas as pl
from jax.experimental.pallas import tpu as pltpu
from jax.sharding import PartitionSpec as P

NB = 1376
RANK = 224
HALF = 128
ROWS = 48
PANELS = 14
LANES = (384, 768, 1152, 1376)
HIGH = lax.Precision.HIGHEST
MESH_ID = pl.DeviceIdType.MESH
VMEM_LIMIT = 56 * 1024 * 1024


def dot_nt(a, b, **kw):
    return lax.dot_general(a, b, (((1,), (1,)), ((), ())), preferred_element_type=jnp.float32, **kw)


def dot_nn(a, b, **kw):
    return lax.dot_general(a, b, (((1,), (0,)), ((), ())), preferred_element_type=jnp.float32, **kw)


def prepare_kernel(row_rank, col_rank, diag, ru, rv, cu, cv, rs, cs, ds):
    col = lax.axis_index("col")
    row = lax.axis_index("row")
    zero_row = jnp.zeros((1, NB), jnp.bfloat16)
    spot = lax.broadcasted_iota(jnp.int32, (7, NB), 0)
    for u, v, out, first, count in ((ru, rv, rs, 7 * col, row_rank[0]), (cu, cv, cs, 7 * row, col_rank[0])):
        out[0, 0:7, :] = u[...]
        out[0, 7:8, :] = zero_row
        kept = jnp.where(spot + first < count, v[...].astype(jnp.float32), 0.0)
        out[1, 0:7, :] = kept.astype(jnp.bfloat16)
        out[1, 7:8, :] = zero_row
    ds[0:43, :] = diag[...]
    ds[43:48, :] = jnp.zeros((5, NB), jnp.bfloat16)


def prepare(row_rank, col_rank, diag, ru, rv, cu, cv):
    vmem = pl.BlockSpec(memory_space=pltpu.VMEM)
    return pl.pallas_call(
        prepare_kernel,
        name="prepare",
        in_specs=[pl.BlockSpec(memory_space=pltpu.SMEM)] * 2 + [vmem] * 5,
        out_specs=[vmem] * 3,
        out_shape=[
            jax.ShapeDtypeStruct((2, 8, NB), jnp.bfloat16),
            jax.ShapeDtypeStruct((2, 8, NB), jnp.bfloat16),
            jax.ShapeDtypeStruct((ROWS, NB), jnp.bfloat16),
        ],
    )(row_rank, col_rank, diag, ru, rv, cu, cv)


def gather_kernel(rs, cs, ds, r_all, c_all, d_all, own, quad_s, quad_r, zs, zr, zps, zpr, ys, yr, xs, xr,
                  dxs, dxr, dfs, dfr, dhs, dhr, dbs, ps, pr):
    row, col = lax.axis_index("row"), lax.axis_index("col")
    x, yh = row // 4, row % 4
    z, q = col // 4, col % 4
    low, core = q // 2, q % 2

    def quad(k):
        there = jnp.where(k % 2 == 1, 1 - core, core)
        return jnp.where(k // 2 == 1, 1 - low, low) * 2 + there

    def mate(k):
        return (row, z * 4 + quad(k))

    def along_z(step):
        return (row, (z + step) % 8 * 4 + q)

    def along_y(step):
        return (x * 4 + (yh + step) % 4, col)

    def along_x(step):
        return ((x + step) % 8 * 4 + yh, col)

    def beside(way):
        there = yh + low if way == 0 else yh + low + 3
        return (x * 4 + there % 4, z * 4 + (1 - low) * 2 + core)

    def remote(src, dst, send, recv, device):
        return pltpu.make_async_remote_copy(
            src_ref=src, dst_ref=dst, send_sem=send, recv_sem=recv, device_id=device, device_id_type=MESH_ID
        )

    across_pair = (x * 4 + (yh + 2 * low + 3) % 4, z * 4 + (1 - low) * 2 + core)
    partners = (
        [mate(1), mate(2), mate(3), along_z(1), along_z(7), across_pair]
        + [along_y(1), along_y(2), along_y(3), along_x(1), along_x(2), along_x(6), along_x(7)]
    )
    barrier = pltpu.get_barrier_semaphore()
    for device in partners:
        pl.semaphore_signal(barrier, inc=1, device_id=device, device_id_type=MESH_ID)
    local = [
        pltpu.make_async_copy(cs, c_all.at[x, yh], own.at[0]),
        pltpu.make_async_copy(ds, d_all.at[x, yh], own.at[1]),
        pltpu.make_async_copy(rs, r_all.at[z, q], own.at[2]),
    ]
    for copy in local:
        copy.start()
    pl.semaphore_wait(barrier, len(partners))

    ends = []

    def go(copy):
        copy.start()
        ends.append(copy.wait_send)

    def by_class(xo, act):
        for k, lanes in enumerate(LANES):
            @pl.when(xo // 2 == k)
            def _(lanes=lanes):
                act(lanes)

    def origin(here, way, step):
        return (here + (8 - step if way == 0 else step)) % 8

    def z_length(way, k):
        return 4 if (k == 0) == (way == 0) else 3

    def z_copy(way, step, k):
        slot = r_all.at[origin(z, way, step), quad(k)]
        src = rs if step == 0 and k == 0 else slot
        return remote(src, slot, zs.at[way, step, k // 2], zr.at[way, step, k // 2], along_z(1 if way == 0 else 7))

    def z_tick(step):
        for k in (0, 2):
            if step == 0 and k == 2:
                remote(rs, r_all.at[z, quad(2)], quad_s.at[2], quad_r.at[2], mate(2)).wait_recv()
            for way in (0, 1):
                if 1 <= step <= z_length(way, k):
                    slot = r_all.at[origin(z, way, step), quad(k)]
                    remote(slot, slot, zs.at[way, step - 1, k // 2], zr.at[way, step - 1, k // 2], mate(1)).wait_recv()
                if step < z_length(way, k):
                    go(z_copy(way, step, k))
                if 1 <= step <= z_length(way, k):
                    sems = (zps.at[way, step - 1, k // 2], zpr.at[way, step - 1, k // 2])
                    go(remote(slot, slot, *sems, mate(1)))
                    theirs = r_all.at[origin(z, way, step), quad(k + 1)]
                    ends.append(remote(theirs, theirs, *sems, mate(1)).wait_recv)

    def x_length(way, t):
        return 4 if (t % 2 == 1) == (way == 0) else 3

    def x_tick(t, step):
        if step == 0 and t > 0:
            remote(cs, c_all.at[x, (yh + 4 - t) % 4], ys.at[t], yr.at[t], along_y(t)).wait_recv()
        for way in (0, 1):
            slot = c_all.at[origin(x, way, step), (yh + 4 - t) % 4]
            ahead = along_x(1 if way == 0 else 7)
            if 1 <= step <= x_length(way, t):
                remote(slot, slot, xs.at[way, step - 1, t], xr.at[way, step - 1, t], ahead).wait_recv()
            if step < x_length(way, t):
                src = cs if step == 0 and t == 0 else slot
                go(remote(src, slot, xs.at[way, step, t], xr.at[way, step, t], ahead))

    chunks = [(0, 0), (0, 1), (1, 1), (0, 2), (1, 2), (0, 3), (1, 3), (0, 4)]

    def d_part(xo, there, half, lanes):
        return d_all.at[xo, there % 4, half, :, pl.ds(0, lanes)]

    def d_run(method, j, there, send, recv, device, mine=False):
        xo = origin(x, *chunks[j])

        def act(lanes):
            part = d_part(xo, there, core, lanes)
            src = ds.at[core, :, pl.ds(0, lanes)] if mine else part
            getattr(remote(src, part, send, recv, device), method)()

        by_class(xo, act)

    def d_send(*args, when=None, **kw):
        if when is None:
            d_run("start", *args, **kw)
            ends.append(lambda: d_run("wait_send", *args, **kw))
        else:
            guarded(low == when, lambda: d_run("start", *args, **kw))
            ends.append(lambda: guarded(low == when, lambda: d_run("wait_send", *args, **kw)))

    def d_wait(j, there, half, send, recv):
        xo = origin(x, *chunks[j])

        def act(lanes):
            part = d_part(xo, there, half, lanes)
            remote(part, part, send, recv, mate(1)).wait_recv()

        by_class(xo, act)

    def share(j, there, index):
        sems = (ps.at[index, j], pr.at[index, j])
        d_send(j, there, *sems, mate(1))
        ends.append(lambda: d_wait(j, there, 1 - core, *sems))

    def guarded(condition, act):
        @pl.when(condition)
        def _():
            act()

    def y_send(way, j, full, when):
        base = yh + low + 3 if way == 0 else yh + low
        if full:
            mine = j == 0 and when == 1 - way
            d_send(j, base, dfs.at[way, j], dfr.at[way, j], beside(way), when=when, mine=mine)
        else:
            there = base + 3 if way == 0 else base + 1
            beyond = along_y(1 if way == 0 else 3)
            d_send(j, there, dbs.at[way, j], dhr.at[way, j], beyond, when=when)
            d_send(j, there, dhs.at[way, j], dhr.at[way, j], beside(way), when=when)

    def late_share(j, there, index, when):
        sems = (ps.at[index, j], pr.at[index, j])
        d_send(j, there, *sems, mate(1), when=when)
        ends.append(lambda: guarded(low == when, lambda: d_wait(j, there, 1 - core, *sems)))

    reached = [0, 1, 1, 1, 1, 2, 2, 2]

    def y_tick(tick):
        order = sorted(range(8), key=lambda j: reached[j])
        for hop in (0, 1, 2, 3):
            for j in order:
                if tick - reached[j] != hop:
                    continue
                for way in (0, 1):
                    first = 1 - way
                    half = j % 2 == way
                    beside_pair = yh + 3 if way == 0 else yh + 1
                    if hop == 0:
                        y_send(way, j, True, first)
                    elif hop in (1, 2):
                        here = 1 - first if hop == 1 else first
                        guarded(
                            low == here,
                            lambda: d_wait(j, beside_pair, core, dfs.at[way, j], dfr.at[way, j]),
                        )
                        if hop == 1:
                            y_send(way, j, True, here)
                        elif half:
                            y_send(way, j, False, here)
                        late_share(j, beside_pair, 1 + way, here)
                    elif half:
                        d_wait(j, yh + 2, core, dhs.at[way, j], dhr.at[way, j])
                        share(j, yh + 2, 3)

    def dx_send(way, far, step, mine):
        j = 0 if mine else chunks.index((way, 2))
        d_send(
            j, yh, dxs.at[way, far - 1], dxr.at[way, far - 1], along_x(step if way == 0 else 8 - step), mine=mine
        )

    def dx_wait(way, far):
        d_wait(chunks.index((way, far)), yh, core, dxs.at[way, far - 1], dxr.at[way, far - 1])

    def dx_tick(tick):
        if tick == 0:
            for way in (0, 1):
                dx_send(way, 2, 2, True)
            for way in (0, 1):
                dx_send(way, 1, 1, True)
        if tick == 1:
            dx_wait(0, 2)
            dx_send(0, 4, 2, False)
            dx_send(0, 3, 1, False)
            dx_wait(1, 2)
            dx_send(1, 3, 1, False)
            for way in (0, 1):
                dx_wait(way, 1)
        if tick == 2:
            for way in (0, 1):
                dx_wait(way, 3)
            dx_wait(0, 4)
        for j in range(1, 8):
            if reached[j] == tick:
                share(j, yh, 0)

    for t in (1, 2, 3):
        go(remote(cs, c_all.at[x, yh], ys.at[t], yr.at[t], along_y(t)))
    for k in (2, 1, 3):
        copy = remote(rs, r_all.at[z, q], quad_s.at[k], quad_r.at[k], mate(k))
        go(copy)
        if k != 2:
            theirs = r_all.at[z, quad(k)]
            ends.append(remote(theirs, theirs, quad_s.at[k], quad_r.at[k], mate(k)).wait_recv)
    for tick in range(6):
        if tick <= 2:
            dx_tick(tick)
        y_tick(tick)
        if tick <= 4:
            x_tick(0, tick)
            z_tick(tick)
            for t in (1, 3, 2):
                x_tick(t, tick)
    for wait in ends:
        wait()
    for copy in local:
        copy.wait()


def gather(rs, cs, ds):
    dma = pltpu.SemaphoreType.DMA
    anywhere = pl.BlockSpec(memory_space=pl.ANY)
    return pl.pallas_call(
        gather_kernel,
        name="gather",
        in_specs=[anywhere] * 3,
        out_specs=[anywhere] * 3,
        out_shape=[
            jax.ShapeDtypeStruct((8, 4, 2, 8, NB), jnp.bfloat16),
            jax.ShapeDtypeStruct((8, 4, 2, 8, NB), jnp.bfloat16),
            jax.ShapeDtypeStruct((8, 4, 2, ROWS // 2, NB), jnp.bfloat16),
        ],
        scratch_shapes=[
            dma((3,)), dma((4,)), dma((4,)), dma((2, 4, 2)), dma((2, 4, 2)), dma((2, 4, 2)), dma((2, 4, 2)),
            dma((4,)), dma((4,)), dma((2, 4, 4)), dma((2, 4, 4)), dma((2, 4)), dma((2, 4)),
            dma((2, 8)), dma((2, 8)), dma((2, 8)), dma((2, 8)), dma((2, 8)), dma((4, 8)), dma((4, 8)),
        ],
        compiler_params=pltpu.CompilerParams(collective_id=0, has_side_effects=True),
    )(rs, cs, ds)


def inverse_factor(gram):
    a = [gram[8 * i : 8 * i + 8, :] for i in range(PANELS)]
    lane = lax.broadcasted_iota(jnp.int32, (8, HALF), 1)
    line = lax.broadcasted_iota(jnp.int32, (8, HALF), 0)
    w = [jnp.where(lane == line + 8 * i, 1.0, 0.0).astype(jnp.float32) for i in range(PANELS)]
    done = []
    for k in range(PANELS):
        at = 8 * k
        d = [[jnp.broadcast_to(a[k][i : i + 1, at + j : at + j + 1], (8, HALF)) for j in range(i + 1)] for i in range(8)]
        low = [[None] * 8 for _ in range(8)]
        inv = []
        for j in range(8):
            inv.append(lax.rsqrt(d[j][j]))
            for i in range(j + 1, 8):
                low[i][j] = d[i][j] * inv[j]
            for i in range(j + 1, 8):
                for m in range(j + 1, i + 1):
                    d[i][m] = d[i][m] - low[i][j] * low[m][j]
        rows_a = [jnp.broadcast_to(a[k][i : i + 1, :], (8, HALF)) for i in range(8)]
        rows_w = [jnp.broadcast_to(w[k][i : i + 1, :], (8, HALF)) for i in range(8)]
        for j in range(8):
            rows_a[j] = rows_a[j] * inv[j]
            rows_w[j] = rows_w[j] * inv[j]
            for i in range(j + 1, 8):
                rows_a[i] = rows_a[i] - low[i][j] * rows_a[j]
                rows_w[i] = rows_w[i] - low[i][j] * rows_w[j]
        for i in range(k + 1, PANELS):
            cols = [jnp.broadcast_to(a[i][:, at + j : at + j + 1], (8, HALF)) for j in range(8)]
            for j in range(8):
                cols[j] = cols[j] * inv[j]
                for m in range(j + 1, 8):
                    cols[m] = cols[m] - cols[j] * low[m][j]
                a[i] = a[i] - cols[j] * rows_a[j]
                w[i] = w[i] - cols[j] * rows_w[j]
        final = rows_w[0]
        for j in range(1, 8):
            final = jnp.where(line == j, rows_w[j], final)
        done.append(final)
    done.append(jnp.zeros((HALF - 8 * PANELS, HALF), jnp.float32))
    return jnp.concatenate(done, axis=0)


def update_kernel(old_rank, new_rank, r_all, c_all, d_all, tu, tv, sk, new_u, new_v, solved, range_y):
    bf = jnp.bfloat16
    f32 = jnp.float32
    old_count, new_count = old_rank[0, 0], new_rank[0, 0]
    ru = r_all[:, 0].reshape(256, NB)
    rv = r_all[:, 1].reshape(256, NB)
    cu = c_all[:, 0].reshape(256, NB)
    cv = c_all[:, 1].reshape(256, NB)
    new_line = lax.broadcasted_iota(jnp.int32, (HALF, NB), 0)
    probe = jnp.where(new_line < new_count, sk[0:HALF, :].astype(f32), 0.0).astype(bf)
    old_keep = lax.broadcasted_iota(jnp.int32, (HALF, RANK), 1) < old_count
    left_small = jnp.where(old_keep, dot_nt(probe, tv[...]), 0.0).astype(bf)
    across = dot_nt(probe, cu).astype(bf)
    base = dot_nn(left_small, tu[...])
    vs = jnp.concatenate([rv, cv], axis=0)
    for xo in range(8):
        lanes = LANES[xo // 2]
        block = d_all[xo, :, :, 0:lanes].reshape(4 * ROWS, lanes)
        solved[:, pl.ds(4 * ROWS * xo, 4 * ROWS)] = dot_nt(vs[:, 0:lanes], block).astype(bf)
    core = dot_nt(solved[0:256, :], solved[256:512, :]).astype(bf)
    middle = dot_nt(across, core).astype(bf)
    y = base - dot_nn(middle, ru)
    range_y[...] = y
    gram = dot_nt(y, y, precision=HIGH)
    lane = lax.broadcasted_iota(jnp.int32, (HALF, HALF), 1)
    line = lax.broadcasted_iota(jnp.int32, (HALF, HALF), 0)
    gram = gram + jnp.where((lane == line) & (line >= new_count), 1.0, 0.0)
    inverse = inverse_factor(gram)
    u = (jnp.sqrt(f32(NB)) * dot_nn(inverse, range_y[...], precision=HIGH)).astype(bf)
    new_u[0:HALF, :] = u
    new_u[HALF:RANK, :] = jnp.zeros((RANK - HALF, NB), bf)
    back = jnp.where(old_keep, dot_nt(u, tu[...]), 0.0).astype(bf)
    side = dot_nt(u, ru).astype(bf)
    turned = dot_nn(side, core).astype(bf)
    new_v[0:HALF, :] = ((dot_nn(back, tv[...]) - dot_nn(turned, cu)) / f32(NB)).astype(bf)
    new_v[HALF:RANK, :] = jnp.zeros((RANK - HALF, NB), bf)


def update(old_rank, new_rank, r_all, c_all, d_all, tu, tv, sk):
    vmem = pl.BlockSpec(memory_space=pltpu.VMEM)
    out = jax.ShapeDtypeStruct((RANK, NB), jnp.bfloat16)
    return pl.pallas_call(
        update_kernel,
        name="update",
        in_specs=[pl.BlockSpec(memory_space=pltpu.SMEM)] * 2 + [vmem] * 6,
        out_specs=[vmem] * 2,
        out_shape=[out, out],
        scratch_shapes=[pltpu.VMEM((512, 32 * ROWS), jnp.bfloat16), pltpu.VMEM((HALF, NB), jnp.float32)],
        compiler_params=pltpu.CompilerParams(vmem_limit_bytes=VMEM_LIMIT),
    )(old_rank, new_rank, r_all.reshape(32, 2, 8, NB), c_all.reshape(32, 2, 8, NB), d_all.reshape(8, 4, ROWS, NB), tu, tv, sk)


def on_device(diag_inverse, row_u, row_v, col_u, col_v, tile_u, tile_v, sketch, row_rank, col_rank, old_rank, new_rank):
    rs, cs, ds = prepare(row_rank, col_rank, diag_inverse, row_u[0].T, row_v[0].T, col_u[0].T, col_v[0].T)
    r_all, c_all, d_all = gather(rs, cs, ds.reshape(2, ROWS // 2, NB))
    new_u, new_v = update(old_rank, new_rank, r_all, c_all, d_all, tile_u[0, 0].T, tile_v[0, 0].T, sketch.T)
    return (new_u.T[None, None], new_v.T[None, None])


def solution(mesh):
    in_specs = (
        P("row", None),
        P("row", None, "col"),
        P("row", None, "col"),
        P("col", None, "row"),
        P("col", None, "row"),
        P("row", "col", None, None),
        P("row", "col", None, None),
        P(),
        P("row"),
        P("col"),
        P("row", "col"),
        P("row", "col"),
    )
    out_specs = (P("row", "col", None, None), P("row", "col", None, None))
    return jax.shard_map(
        on_device, mesh=mesh, in_specs=in_specs, out_specs=out_specs, check_vma=False
    )
```
